32 devices in a mesh: groups: 1, samp: 4 (over x, core), var: 8 (over z, y).
Axes of the slice: x: 2, y: 2, z: 4, core: 2. Of those that a mesh axis runs over, the one named last changes fastest.
Arguments:
- expression: bfloat16 [4096, 5120], P(('groups', 'samp'), 'var'), may hold values from -6 to 6
- genotypes: bfloat16 [4096, 1536], P(('groups', 'samp'), 'var'), may hold values from 0 to 2
- covariates: bfloat16 [4096, 64], P(('groups', 'samp')), may hold values from -6 to 6
- distance_bins: int32 [24, 5120], P('groups', ('var', 'samp')), may hold values from 0 to 15
- gene_folds: int32 [5120], P(('groups', 'var', 'samp')), may hold values from 0 to 4
- fold_weights: float32 [5, 16], replicated, may hold values from 0.25 to 4
Outputs:
- weighted_stats: float32 [5120, 1536], P(('groups', 'var', 'samp'))
The draws below stay inside these ranges and needn't reach their ends.
Inputs may be any that keep to these rules, and one draw needn't show every extreme that they name: `distance_bins`: bins index rows of fold_weights' second dimension. `gene_folds`: folds index rows of fold_weights.
All inputs are finite; a program needn't handle non-finite values.
Results may differ from the reference program's by a relative error of at most 0.0047.
Values may be sent and summed in bfloat16 or wider, within the bound.
A program may use at most 64 MiB of HBM per device.

```python
import math
import jax
import jax.numpy as jnp
from jax import lax

COVS = 64
VARS = 1536
VTILE = 64
NBINS = 16
FOLDS = 5
SAMPLES = 4096
GENES = 5120
VTILES = 24


def set_ends(values, rng, low, largest):
    dims = values.shape
    spot = [jax.random.randint(jax.random.fold_in(rng, axis), (), 0, dims[axis]) for axis in range(len(dims))]
    values = values.at[tuple(spot)].set(low)
    longest = dims.index(max(dims))
    spot[longest] = (spot[longest] + 1) % dims[longest]
    return values.at[tuple(spot)].set(largest)


def block_scale(own_key, extent, split, low, top_value):
    def one(position, blocks):
        steps = jax.random.uniform(jax.random.fold_in(jax.random.fold_in(own_key, 6), position), (blocks,), jnp.float32, low / len(split), top_value / len(split))
        return jnp.repeat(jnp.exp(steps), extent[position] // blocks).reshape((-1,) + (1,) * (len(extent) - position - 1))

    level = one(*split[0])
    for cut in split[1:]:
        level = level * one(*cut)
    return level


def bell_draw(rng, dims, spread, limit, pieces=(), dtype=jnp.bfloat16):
    drawn = spread * jax.random.normal(rng, dims, jnp.float32)
    if pieces:
        drawn = drawn * block_scale(rng, dims, pieces, -0.22, 0.18)
    return jnp.clip(drawn, -limit, limit).astype(dtype)


def setup_inputs(seed: int = 0, part: int = 0) -> dict:
    streams_of = jax.random.split(jax.random.key(seed), 7)
    part_splits = jax.random.split(jax.random.fold_in(streams_of[6], part), 7)
    expression = bell_draw(part_splits[0], (SAMPLES, GENES), 1.0, 6.0, ((0, 4), (1, 8)))
    genotypes = jnp.clip(2.0 * jax.random.uniform(part_splits[1], (SAMPLES, VARS), jnp.float32) ** block_scale(part_splits[1], (SAMPLES, VARS), ((0, 4), (1, 8)), -0.2, 0.2), 0.0, 2.0).astype(jnp.bfloat16)
    covariates = bell_draw(part_splits[2], (SAMPLES, COVS), 1.0, 6.0, ((0, 4),))
    distance_bins = set_ends(jax.random.randint(part_splits[3], (VTILES, GENES), 0, NBINS), jax.random.fold_in(part_splits[3], 1), 0, NBINS - 1).astype(jnp.int32)
    gene_folds = set_ends(jax.random.randint(part_splits[4], (GENES,), 0, FOLDS), jax.random.fold_in(part_splits[4], 1), 0, FOLDS - 1).astype(jnp.int32)
    fold_weights = jnp.clip(jnp.exp(jax.random.uniform(streams_of[5], (FOLDS, NBINS), jnp.float32, math.log(0.25), math.log(4.0))), 0.25, 4.0)
    return dict(expression=expression, genotypes=genotypes, covariates=covariates, distance_bins=distance_bins, gene_folds=gene_folds, fold_weights=fold_weights)


def standardize(data, design, gram):
    cross = jnp.dot(design.T.astype(jnp.float32), data.astype(jnp.float32), preferred_element_type=jnp.float32)
    beta = jnp.linalg.solve(gram, cross)
    fitted = jnp.dot(design.astype(jnp.float32), beta, precision=lax.Precision.HIGHEST)
    residual = data.astype(jnp.float32) - fitted
    norm = lax.optimization_barrier(jnp.sum(residual * residual, axis=0))
    return (residual * lax.rsqrt(norm + 1e-06)).astype(jnp.bfloat16)

def reference(expression, genotypes, covariates, distance_bins, gene_folds, fold_weights):
    samples = expression.shape[0]
    design = jnp.concatenate([jnp.ones((samples, 1), jnp.bfloat16), covariates], axis=1)
    gram = jnp.dot(design.T.astype(jnp.float32), design.astype(jnp.float32), preferred_element_type=jnp.float32)
    expr_unit = standardize(expression, design, gram)
    geno_unit = standardize(genotypes, design, gram)
    corr = jnp.dot(expr_unit.T.astype(jnp.float32), geno_unit.astype(jnp.float32), preferred_element_type=jnp.float32)
    row_weights = fold_weights[gene_folds]
    tile_weight = jnp.take_along_axis(row_weights, distance_bins.T, axis=1)
    dof = jnp.float32(samples - COVS - 2)
    stats = dof * corr * corr
    genes = corr.shape[0]
    weighted = stats.reshape(genes, VTILES, VTILE) * tile_weight[:, :, None]
    return weighted.reshape(genes, VARS)
```

```python
import functools
import math
import jax
import jax.numpy as jnp
from jax import lax
from jax.experimental import pallas as pl
from jax.experimental.pallas import tpu as pltpu
from jax.sharding import PartitionSpec as P

COVS = 64
VARS = 1536
VTILE = 64
NBINS = 16
FOLDS = 5
VTILES = 24
LANES = 128
MESH = pl.DeviceIdType.MESH
NT = (((1,), (1,)), ((), ()))
NN = (((1,), (0,)), ((), ()))


def round_up(size, step):
    return -(-size // step) * step


DESIGN = COVS + 1
DROWS = round_up(DESIGN, 8)


def remote(src, dst, send, recv, axis, peer):
    return pltpu.make_async_remote_copy(
        src_ref=src, dst_ref=dst, send_sem=send, recv_sem=recv,
        device_id={axis: peer}, device_id_type=MESH,
    )


def invert(gram):
    rows = lax.broadcasted_iota(jnp.int32, gram.shape, 0)
    cols = lax.broadcasted_iota(jnp.int32, gram.shape, 1)
    valid = (rows < DESIGN) & (cols < DESIGN)
    start = jnp.where(valid, gram, 0.0)

    def sweep(k, a):
        row = jnp.sum(jnp.where(rows == k, a, 0.0), axis=0, keepdims=True)
        col = jnp.sum(jnp.where(cols == k, a, 0.0), axis=1, keepdims=True)
        pivot = jnp.sum(jnp.where(cols[:1] == k, row, 0.0), axis=1, keepdims=True)
        inv = 1.0 / pivot
        scaled = row * inv
        a = jnp.where(cols == k, 0.0, a) - col * jnp.where(cols[:1] == k, inv, scaled)
        return jnp.where(rows == k, jnp.where(cols[:1] == k, inv, scaled), a)

    swept = lax.fori_loop(0, DESIGN, sweep, start)
    return jnp.where(valid, swept, 0.0)


def kernel(S, V, xe_ref, xg_ref, gt_ref, d_ref, out_ref,
           gbuf, bbuf, btile, bsend, gram_own, gram_in, cross_own, cross_in,
           resid, norm_own, norm_in, norm_cols, unit, source, terms, terms_in,
           gs, gr, bs, br, ms, mr, cs, cr, ns, nr, ts, tr):
    me = lax.axis_index("var")
    mine = lax.axis_index("samp")
    genes, samples = xe_ref.shape
    vb = gt_ref.shape[0]
    etiles = genes // LANES
    gtiles = xg_ref.shape[0] // LANES
    tiles = etiles + gtiles
    groups, group = terms.shape[0], terms.shape[2] // vb
    chunk = genes // S

    def var_peer(k):
        return lax.rem(me + k, V)

    def samp_peer(k):
        return lax.rem(mine + k, S)

    barrier = pltpu.get_barrier_semaphore()
    for k in range(1, V):
        pl.semaphore_signal(barrier, inc=1, device_id={"var": var_peer(k)}, device_id_type=MESH)
    for k in range(1, S):
        pl.semaphore_signal(barrier, inc=1, device_id={"samp": samp_peer(k)}, device_id_type=MESH)
    gram = lax.dot_general(d_ref[...], d_ref[...], NT, preferred_element_type=jnp.float32)
    gram_own[...] = gram[:DROWS]
    norm_own[...] = jnp.zeros_like(norm_own)
    pl.semaphore_wait(barrier, V + S - 2)

    def block_copy(k):
        return remote(gt_ref, gbuf.at[me], gs.at[k], gr.at[me], "var", var_peer(k))

    def gram_copy(k):
        return remote(gram_own, gram_in.at[mine], ms.at[k], mr.at[mine], "samp", samp_peer(k))

    def cross_copy(k):
        return remote(cross_own, cross_in.at[mine], cs.at[k], cr.at[mine], "samp", samp_peer(k))

    def norm_copy(k):
        return remote(norm_own, norm_in.at[mine], ns.at[k], nr.at[mine], "samp", samp_peer(k))

    def beta_copy(k):
        return remote(bsend, bbuf.at[me], bs.at[k], br.at[me], "var", var_peer(k))

    for k in range(1, S):
        gram_copy(k).start()
    for k in range(1, V):
        block_copy(k).start()

    def x_tile(t, use):
        @pl.when(t < etiles)
        def _():
            use(xe_ref[pl.ds(pl.multiple_of(t * LANES, LANES), LANES), :])

        @pl.when(t >= etiles)
        def _():
            use(xg_ref[pl.ds(pl.multiple_of((t - etiles) * LANES, LANES), LANES), :])

    @pl.loop(0, tiles)
    def _(t):
        def use(x):
            full = lax.dot_general(d_ref[...], x, NT, preferred_element_type=jnp.float32)
            cross_own[t] = full[:DROWS]
        x_tile(t, use)

    for k in range(1, S):
        cross_copy(k).start()
    gbuf[me] = gt_ref[...]

    gram_sum = gram_own[...]
    for k in range(1, S):
        p = samp_peer(k)
        remote(gram_own, gram_in.at[p], ms.at[k], mr.at[p], "samp", p).wait_recv()
        gram_sum = gram_sum + gram_in[p]
    inverse = invert(gram_sum)
    inverse = jnp.concatenate([inverse, jnp.zeros((LANES - DROWS, LANES), jnp.float32)], axis=0)

    for k in range(1, S):
        p = samp_peer(k)
        remote(cross_own, cross_in.at[p], cs.at[k], cr.at[p], "samp", p).wait_recv()

    @pl.loop(0, tiles)
    def _(t):
        total = cross_own[t]
        for k in range(1, S):
            total = total + cross_in[samp_peer(k), t]
        padded = jnp.concatenate([total, jnp.zeros((LANES - DROWS, LANES), jnp.float32)], axis=0)
        beta = lax.dot_general(padded.T, inverse, NN, precision=lax.Precision.HIGHEST,
                               preferred_element_type=jnp.float32)
        hi = beta.astype(jnp.bfloat16)
        lo = (beta - hi.astype(jnp.float32)).astype(jnp.bfloat16)
        fitted = lax.dot_general(hi, d_ref[...], NN, preferred_element_type=jnp.float32)
        fitted = fitted + lax.dot_general(lo, d_ref[...], NN, preferred_element_type=jnp.float32)

        def use(x):
            left = x.astype(jnp.float32) - fitted
            resid[t] = left
            square = left * left
            part = square[:, :LANES]
            for c in range(1, samples // LANES):
                part = part + square[:, c * LANES:(c + 1) * LANES]
            norm_own[pl.ds(t, 1), :] = jnp.sum(part.T, axis=0, keepdims=True)
        x_tile(t, use)

        @pl.when(t >= etiles)
        def _():
            btile[t - etiles] = hi

    for k in range(1, S):
        norm_copy(k).start()
    norm = norm_own[...]
    for k in range(1, S):
        p = samp_peer(k)
        remote(norm_own, norm_in.at[p], ns.at[k], nr.at[p], "samp", p).wait_recv()
        norm = norm + norm_in[p]
    norm_cols[...] = lax.rsqrt(norm + 1e-06)

    def column(t):
        row = norm_cols[pl.ds(t, 1), :]
        return jnp.broadcast_to(row, (LANES, LANES)).T

    lanes = lax.broadcasted_iota(jnp.int32, (LANES, LANES), 1)
    for g in range(gtiles):
        col = column(etiles + g)
        hi = col.astype(jnp.bfloat16).astype(jnp.float32)
        lo = col - hi
        message = btile[g].astype(jnp.float32)
        message = jnp.where(lanes == DESIGN, hi, jnp.where(lanes == DESIGN + 1, lo, message))
        rows = min(LANES, vb - g * LANES)
        bsend[pl.ds(g * LANES, rows), :] = message[:rows].astype(jnp.bfloat16)
    for k in range(1, V):
        beta_copy(k).start()
    bbuf[me] = bsend[...]

    @pl.loop(0, etiles)
    def _(t):
        unit[pl.ds(pl.multiple_of(t * LANES, LANES), LANES), :] = (
            resid[t] * column(t)[:, :1]
        ).astype(jnp.bfloat16)

    home = me // group

    @pl.loop(0, groups)
    def _(q):
        slab = lax.rem(home + q, groups)
        for b in range(group):
            v = slab * group + b

            @pl.when(v != me)
            def _():
                remote(gt_ref, gbuf.at[v], gs.at[0], gr.at[v], "var", v).wait_recv()
                remote(bsend, bbuf.at[v], bs.at[0], br.at[v], "var", v).wait_recv()

            fit_in = bbuf[v]
            scale = fit_in[:, DESIGN:DESIGN + 1].astype(jnp.float32)
            scale = scale + fit_in[:, DESIGN + 1:DESIGN + 2].astype(jnp.float32)
            fitted = lax.dot_general(fit_in, d_ref[...], NN, preferred_element_type=jnp.float32)
            source[b * vb:(b + 1) * vb, :] = (
                (gbuf[v].astype(jnp.float32) - fitted) * scale
            ).astype(jnp.bfloat16)

        @pl.loop(0, S)
        def _(i):
            rows = pl.ds(pl.multiple_of(i * chunk, 16), chunk)
            term = lax.dot_general(unit[rows, :], source[...], NT, preferred_element_type=jnp.float32)
            terms[slab, rows, :] = term.astype(jnp.bfloat16)

        for k in range(1, S):
            p = samp_peer(k)
            part = terms.at[slab, pl.ds(pl.multiple_of(p * chunk, 16), chunk)]
            remote(part, terms_in.at[slab, mine], ts.at[slab, k], tr.at[slab, mine], "samp", p).start()

    width = group * vb
    own_rows = pl.ds(pl.multiple_of(mine * chunk, 16), chunk)

    @pl.loop(0, groups)
    def _(q):
        slab = lax.rem(home + q, groups)
        total = terms[slab, own_rows, :].astype(jnp.float32)
        for k in range(1, S):
            p = samp_peer(k)
            remote(terms.at[slab, own_rows], terms_in.at[slab, p], ts.at[slab, k], tr.at[slab, p],
                   "samp", p).wait_recv()
            total = total + terms_in[slab, p].astype(jnp.float32)
        out_ref[:, pl.ds(pl.multiple_of(slab * width, LANES), width)] = total

    for k in range(1, S):
        gram_copy(k).wait_send()
        cross_copy(k).wait_send()
        norm_copy(k).wait_send()
    for k in range(1, V):
        block_copy(k).wait_send()
        beta_copy(k).wait_send()

    @pl.loop(0, groups)
    def _(slab):
        for k in range(1, S):
            remote(terms.at[slab, own_rows], terms_in.at[slab, mine], ts.at[slab, k],
                   tr.at[slab, mine], "samp", samp_peer(k)).wait_send()


def correlate(expression, genotypes, covariates):
    S, V = lax.axis_size("samp"), lax.axis_size("var")
    samples, genes = expression.shape
    vb = genotypes.shape[1]
    gp = round_up(vb, LANES)
    group = math.lcm(vb, LANES) // vb
    groups = V // group
    tiles = (genes + gp) // LANES
    nrows = round_up(tiles, 8)
    design = jnp.concatenate(
        [jnp.ones((1, samples), jnp.bfloat16), covariates.T,
         jnp.zeros((LANES - DESIGN, samples), jnp.bfloat16)], axis=0)
    gt = genotypes.T
    xg = jnp.pad(gt, ((0, gp - vb), (0, 0)))
    chunk = genes // S
    bf, f32 = jnp.bfloat16, jnp.float32
    dma = pltpu.SemaphoreType.DMA
    return pl.pallas_call(
        functools.partial(kernel, S, V),
        out_shape=jax.ShapeDtypeStruct((chunk, V * vb), f32),
        in_specs=[pl.BlockSpec(memory_space=pltpu.VMEM)] * 4,
        out_specs=pl.BlockSpec(memory_space=pltpu.VMEM),
        scratch_shapes=[
            pltpu.VMEM((V, vb, samples), bf),
            pltpu.VMEM((V, vb, LANES), bf),
            pltpu.VMEM((gp // LANES, LANES, LANES), bf),
            pltpu.VMEM((vb, LANES), bf),
            pltpu.VMEM((DROWS, LANES), f32),
            pltpu.VMEM((S, DROWS, LANES), f32),
            pltpu.VMEM((tiles, DROWS, LANES), f32),
            pltpu.VMEM((S, tiles, DROWS, LANES), f32),
            pltpu.VMEM((tiles, LANES, samples), f32),
            pltpu.VMEM((nrows, LANES), f32),
            pltpu.VMEM((S, nrows, LANES), f32),
            pltpu.VMEM((nrows, LANES), f32),
            pltpu.VMEM((genes, samples), bf),
            pltpu.VMEM((group * vb, samples), bf),
            pltpu.VMEM((groups, genes, group * vb), bf),
            pltpu.VMEM((groups, S, chunk, group * vb), bf),
            dma((V,)), dma((V,)), dma((V,)), dma((V,)),
            dma((S,)), dma((S,)), dma((S,)), dma((S,)), dma((S,)), dma((S,)),
            dma((groups, S)), dma((groups, S)),
        ],
        compiler_params=pltpu.CompilerParams(
            collective_id=0, has_side_effects=True, vmem_limit_bytes=60 * 1024 * 1024),
    )(expression.T, xg, gt, design)


def shards(expression, genotypes, covariates, distance_bins, gene_folds, fold_weights):
    samples = expression.shape[0] * lax.axis_size("samp")
    corr = correlate(expression, genotypes, covariates)
    local_genes = corr.shape[0]
    fold_onehot = (gene_folds[:, None] == jnp.arange(FOLDS)[None, :]).astype(jnp.float32)
    row_weights = jnp.dot(fold_onehot, fold_weights, precision=lax.Precision.HIGHEST)
    bin_match = distance_bins.T[:, :, None] == jnp.arange(NBINS)[None, None, :]
    tile_weight = jnp.sum(jnp.where(bin_match, row_weights[:, None, :], 0.0), axis=2)
    dof = jnp.float32(samples - COVS - 2)
    stats = dof * corr * corr
    weighted = stats.reshape(local_genes, VTILES, VTILE) * tile_weight[:, :, None]
    return weighted.reshape(local_genes, VARS)


def solution(mesh):
    return jax.shard_map(
        shards,
        mesh=mesh,
        in_specs=(
            P(("groups", "samp"), "var"),
            P(("groups", "samp"), "var"),
            P(("groups", "samp"), None),
            P("groups", ("var", "samp")),
            P(("groups", "var", "samp")),
            P(),
        ),
        out_specs=P(("groups", "var", "samp"), None),
        check_vma=False,
    )
```

```python
import functools
import math
import jax
import jax.numpy as jnp
from jax import lax
from jax.experimental import pallas as pl
from jax.experimental.pallas import tpu as pltpu
from jax.sharding import PartitionSpec as P

COVS = 64
VARS = 1536
VTILE = 64
NBINS = 16
FOLDS = 5
VTILES = 24
LANES = 128
MESH = pl.DeviceIdType.MESH
NT = (((1,), (1,)), ((), ()))
NN = (((1,), (0,)), ((), ()))


def round_up(size, step):
    return -(-size // step) * step


DESIGN = COVS + 1
DROWS = round_up(DESIGN, 8)


def remote(src, dst, send, recv, axis, peer):
    return pltpu.make_async_remote_copy(
        src_ref=src, dst_ref=dst, send_sem=send, recv_sem=recv,
        device_id={axis: peer}, device_id_type=MESH,
    )


def invert(gram):
    rows = lax.broadcasted_iota(jnp.int32, gram.shape, 0)
    cols = lax.broadcasted_iota(jnp.int32, gram.shape, 1)
    valid = (rows < DESIGN) & (cols < DESIGN)
    start = jnp.where(valid, gram, 0.0)

    swept = start
    for k in range(DESIGN):
        inv = 1.0 / swept[k:k + 1, k:k + 1]
        col = swept[:, k:k + 1]
        scaled = jnp.where(cols[:1] == k, inv, swept[k:k + 1, :] * inv)
        swept = jnp.where(rows == k, scaled, jnp.where(cols == k, 0.0, swept) - col * scaled)
    return jnp.where(valid, swept, 0.0)


def kernel(S, V, xe_ref, xg_ref, gt_ref, d_ref, out_ref,
           gbuf, bbuf, btile, bsend, gram_own, gram_in, cross_own, cross_in,
           resid, norm_own, norm_in, norm_cols, unit, source, terms, terms_in,
           gs, gr, bs, br, ms, mr, cs, cr, ns, nr, ts, tr):
    me = lax.axis_index("var")
    mine = lax.axis_index("samp")
    genes, samples = xe_ref.shape
    vb = gt_ref.shape[0]
    etiles = genes // LANES
    gtiles = xg_ref.shape[0] // LANES
    tiles = etiles + gtiles
    groups, group = terms.shape[0], terms.shape[2] // vb
    chunk = genes // S

    def var_peer(k):
        return lax.rem(me + k, V)

    def samp_peer(k):
        return lax.rem(mine + k, S)

    barrier = pltpu.get_barrier_semaphore()
    for k in range(1, V):
        pl.semaphore_signal(barrier, inc=1, device_id={"var": var_peer(k)}, device_id_type=MESH)
    for k in range(1, S):
        pl.semaphore_signal(barrier, inc=1, device_id={"samp": samp_peer(k)}, device_id_type=MESH)
    gram = lax.dot_general(d_ref[...], d_ref[...], NT, preferred_element_type=jnp.float32)
    gram_own[...] = gram[:DROWS]
    norm_own[...] = jnp.zeros_like(norm_own)
    pl.semaphore_wait(barrier, V + S - 2)

    def block_copy(k):
        return remote(gt_ref, gbuf.at[me], gs.at[k], gr.at[me], "var", var_peer(k))

    def gram_copy(k):
        return remote(gram_own, gram_in.at[mine], ms.at[k], mr.at[mine], "samp", samp_peer(k))

    def cross_copy(k):
        return remote(cross_own, cross_in.at[mine], cs.at[k], cr.at[mine], "samp", samp_peer(k))

    def norm_copy(k):
        return remote(norm_own, norm_in.at[mine], ns.at[k], nr.at[mine], "samp", samp_peer(k))

    def beta_copy(k):
        return remote(bsend, bbuf.at[me], bs.at[k], br.at[me], "var", var_peer(k))

    for k in range(1, S):
        gram_copy(k).start()
    for k in range(1, V):
        block_copy(k).start()

    def x_tile(t, use):
        @pl.when(t < etiles)
        def _():
            use(xe_ref[pl.ds(pl.multiple_of(t * LANES, LANES), LANES), :])

        @pl.when(t >= etiles)
        def _():
            use(xg_ref[pl.ds(pl.multiple_of((t - etiles) * LANES, LANES), LANES), :])

    @pl.loop(0, tiles)
    def _(t):
        def use(x):
            full = lax.dot_general(d_ref[...], x, NT, preferred_element_type=jnp.float32)
            cross_own[t] = full[:DROWS]
        x_tile(t, use)

    for k in range(1, S):
        cross_copy(k).start()
    gbuf[me] = gt_ref[...]

    gram_sum = gram_own[...]
    for k in range(1, S):
        p = samp_peer(k)
        remote(gram_own, gram_in.at[p], ms.at[k], mr.at[p], "samp", p).wait_recv()
        gram_sum = gram_sum + gram_in[p]
    inverse = invert(gram_sum)
    inverse = jnp.concatenate([inverse, jnp.zeros((LANES - DROWS, LANES), jnp.float32)], axis=0)

    for k in range(1, S):
        p = samp_peer(k)
        remote(cross_own, cross_in.at[p], cs.at[k], cr.at[p], "samp", p).wait_recv()

    @pl.loop(0, tiles)
    def _(t):
        total = cross_own[t]
        for k in range(1, S):
            total = total + cross_in[samp_peer(k), t]
        padded = jnp.concatenate([total, jnp.zeros((LANES - DROWS, LANES), jnp.float32)], axis=0)
        beta = lax.dot_general(padded.T, inverse, NN, precision=lax.Precision.HIGHEST,
                               preferred_element_type=jnp.float32)
        hi = beta.astype(jnp.bfloat16)
        lo = (beta - hi.astype(jnp.float32)).astype(jnp.bfloat16)
        fitted = lax.dot_general(hi, d_ref[...], NN, preferred_element_type=jnp.float32)
        fitted = fitted + lax.dot_general(lo, d_ref[...], NN, preferred_element_type=jnp.float32)

        def use(x):
            left = x.astype(jnp.float32) - fitted
            resid[t] = left
            square = left * left
            part = square[:, :LANES]
            for c in range(1, samples // LANES):
                part = part + square[:, c * LANES:(c + 1) * LANES]
            norm_own[pl.ds(t, 1), :] = jnp.sum(part.T, axis=0, keepdims=True)
        x_tile(t, use)

        @pl.when(t >= etiles)
        def _():
            btile[t - etiles] = hi

    for k in range(1, S):
        norm_copy(k).start()
    norm = norm_own[...]
    for k in range(1, S):
        p = samp_peer(k)
        remote(norm_own, norm_in.at[p], ns.at[k], nr.at[p], "samp", p).wait_recv()
        norm = norm + norm_in[p]
    norm_cols[...] = lax.rsqrt(norm + 1e-06)

    def column(t):
        row = norm_cols[pl.ds(t, 1), :]
        return jnp.broadcast_to(row, (LANES, LANES)).T

    lanes = lax.broadcasted_iota(jnp.int32, (LANES, LANES), 1)
    for g in range(gtiles):
        col = column(etiles + g)
        hi = col.astype(jnp.bfloat16).astype(jnp.float32)
        lo = col - hi
        message = btile[g].astype(jnp.float32)
        message = jnp.where(lanes == DESIGN, hi, jnp.where(lanes == DESIGN + 1, lo, message))
        rows = min(LANES, vb - g * LANES)
        bsend[pl.ds(g * LANES, rows), :] = message[:rows].astype(jnp.bfloat16)
    for k in range(1, V):
        beta_copy(k).start()
    bbuf[me] = bsend[...]

    @pl.loop(0, etiles)
    def _(t):
        unit[pl.ds(pl.multiple_of(t * LANES, LANES), LANES), :] = (
            resid[t] * column(t)[:, :1]
        ).astype(jnp.bfloat16)

    home = me // group

    @pl.loop(0, groups)
    def _(q):
        slab = lax.rem(home + q, groups)
        for b in range(group):
            v = slab * group + b

            @pl.when(v != me)
            def _():
                remote(gt_ref, gbuf.at[v], gs.at[0], gr.at[v], "var", v).wait_recv()
                remote(bsend, bbuf.at[v], bs.at[0], br.at[v], "var", v).wait_recv()

            fit_in = bbuf[v]
            scale = fit_in[:, DESIGN:DESIGN + 1].astype(jnp.float32)
            scale = scale + fit_in[:, DESIGN + 1:DESIGN + 2].astype(jnp.float32)
            fitted = lax.dot_general(fit_in, d_ref[...], NN, preferred_element_type=jnp.float32)
            source[b * vb:(b + 1) * vb, :] = (
                (gbuf[v].astype(jnp.float32) - fitted) * scale
            ).astype(jnp.bfloat16)

        @pl.loop(0, S)
        def _(i):
            rows = pl.ds(pl.multiple_of(i * chunk, 16), chunk)
            term = lax.dot_general(unit[rows, :], source[...], NT, preferred_element_type=jnp.float32)
            terms[slab, rows, :] = term.astype(jnp.bfloat16)

        for k in range(1, S):
            p = samp_peer(k)
            part = terms.at[slab, pl.ds(pl.multiple_of(p * chunk, 16), chunk)]
            remote(part, terms_in.at[slab, mine], ts.at[slab, k], tr.at[slab, mine], "samp", p).start()

    width = group * vb
    own_rows = pl.ds(pl.multiple_of(mine * chunk, 16), chunk)

    @pl.loop(0, groups)
    def _(q):
        slab = lax.rem(home + q, groups)
        total = terms[slab, own_rows, :].astype(jnp.float32)
        for k in range(1, S):
            p = samp_peer(k)
            remote(terms.at[slab, own_rows], terms_in.at[slab, p], ts.at[slab, k], tr.at[slab, p],
                   "samp", p).wait_recv()
            total = total + terms_in[slab, p].astype(jnp.float32)
        out_ref[:, pl.ds(pl.multiple_of(slab * width, LANES), width)] = total

    for k in range(1, S):
        gram_copy(k).wait_send()
        cross_copy(k).wait_send()
        norm_copy(k).wait_send()
    for k in range(1, V):
        block_copy(k).wait_send()
        beta_copy(k).wait_send()

    @pl.loop(0, groups)
    def _(slab):
        for k in range(1, S):
            remote(terms.at[slab, own_rows], terms_in.at[slab, mine], ts.at[slab, k],
                   tr.at[slab, mine], "samp", samp_peer(k)).wait_send()


def correlate(expression, genotypes, covariates):
    S, V = lax.axis_size("samp"), lax.axis_size("var")
    samples, genes = expression.shape
    vb = genotypes.shape[1]
    gp = round_up(vb, LANES)
    group = math.lcm(vb, LANES) // vb
    groups = V // group
    tiles = (genes + gp) // LANES
    nrows = round_up(tiles, 8)
    design = jnp.concatenate(
        [jnp.ones((1, samples), jnp.bfloat16), covariates.T,
         jnp.zeros((LANES - DESIGN, samples), jnp.bfloat16)], axis=0)
    gt = genotypes.T
    xg = jnp.pad(gt, ((0, gp - vb), (0, 0)))
    chunk = genes // S
    bf, f32 = jnp.bfloat16, jnp.float32
    dma = pltpu.SemaphoreType.DMA
    return pl.pallas_call(
        functools.partial(kernel, S, V),
        out_shape=jax.ShapeDtypeStruct((chunk, V * vb), f32),
        in_specs=[pl.BlockSpec(memory_space=pltpu.VMEM)] * 4,
        out_specs=pl.BlockSpec(memory_space=pltpu.VMEM),
        scratch_shapes=[
            pltpu.VMEM((V, vb, samples), bf),
            pltpu.VMEM((V, vb, LANES), bf),
            pltpu.VMEM((gp // LANES, LANES, LANES), bf),
            pltpu.VMEM((vb, LANES), bf),
            pltpu.VMEM((DROWS, LANES), f32),
            pltpu.VMEM((S, DROWS, LANES), f32),
            pltpu.VMEM((tiles, DROWS, LANES), f32),
            pltpu.VMEM((S, tiles, DROWS, LANES), f32),
            pltpu.VMEM((tiles, LANES, samples), f32),
            pltpu.VMEM((nrows, LANES), f32),
            pltpu.VMEM((S, nrows, LANES), f32),
            pltpu.VMEM((nrows, LANES), f32),
            pltpu.VMEM((genes, samples), bf),
            pltpu.VMEM((group * vb, samples), bf),
            pltpu.VMEM((groups, genes, group * vb), bf),
            pltpu.VMEM((groups, S, chunk, group * vb), bf),
            dma((V,)), dma((V,)), dma((V,)), dma((V,)),
            dma((S,)), dma((S,)), dma((S,)), dma((S,)), dma((S,)), dma((S,)),
            dma((groups, S)), dma((groups, S)),
        ],
        compiler_params=pltpu.CompilerParams(
            collective_id=0, has_side_effects=True, vmem_limit_bytes=60 * 1024 * 1024),
    )(expression.T, xg, gt, design)


def shards(expression, genotypes, covariates, distance_bins, gene_folds, fold_weights):
    samples = expression.shape[0] * lax.axis_size("samp")
    corr = correlate(expression, genotypes, covariates)
    local_genes = corr.shape[0]
    fold_onehot = (gene_folds[:, None] == jnp.arange(FOLDS)[None, :]).astype(jnp.float32)
    row_weights = jnp.dot(fold_onehot, fold_weights, precision=lax.Precision.HIGHEST)
    bin_match = distance_bins.T[:, :, None] == jnp.arange(NBINS)[None, None, :]
    tile_weight = jnp.sum(jnp.where(bin_match, row_weights[:, None, :], 0.0), axis=2)
    dof = jnp.float32(samples - COVS - 2)
    stats = dof * corr * corr
    weighted = stats.reshape(local_genes, VTILES, VTILE) * tile_weight[:, :, None]
    return weighted.reshape(local_genes, VARS)


def solution(mesh):
    return jax.shard_map(
        shards,
        mesh=mesh,
        in_specs=(
            P(("groups", "samp"), "var"),
            P(("groups", "samp"), "var"),
            P(("groups", "samp"), None),
            P("groups", ("var", "samp")),
            P(("groups", "var", "samp")),
            P(),
        ),
        out_specs=P(("groups", "var", "samp"), None),
        check_vma=False,
    )
```
